32 devices in a mesh: dp: 8 (over y, x, core), section: 4 (over z).
Axes of the slice: x: 2, y: 2, z: 4, core: 2. Of those that a mesh axis runs over, the one named last changes fastest.
Arguments:
- acts: bfloat16 [8, 4, 2, 64, 4096], P('dp', 'section'), may hold values from -6 to 6
- weight_v: bfloat16 [4, 4096, 512], P('section'), may hold values from -0.09375 to 0.09375
- weight_o: bfloat16 [4, 512, 4096], P('section'), may hold values from -0.09375 to 0.09375
- top_grad: bfloat16 [8, 2, 64, 4096], P('dp'), may hold values from -6 to 6
- loss_mask: int32 [8, 2, 64], P('dp'), may hold values 0 or 1
- q_prev: float32 [4, 512, 64], P('section'), may hold values from -0.25 to 0.25
Outputs:
- basis: float32 [4, 4096, 64], P('section')
- q_next: float32 [4, 512, 64], P('section')
The draws below stay inside these ranges and needn't reach their ends.
All inputs are finite; a program needn't handle non-finite values. No bound on the sum of `loss_mask` on one device may be relied on, other than what follows from the above.
Results may differ from the reference program's by a relative error of at most 0.01.
Values may be sent and summed in bfloat16 or wider, within the bound.
A program may use at most 128 MiB of HBM per device.

```python
import math
import jax
import jax.numpy as jnp
from jax import lax

D = 4096
VW = 512
R = 64
MB = 2
TOK = 64
N_DP = 8
N_SECTION = 4


def with_ends(drawn, rng, low, top_value):
    extent = drawn.shape
    spot = [jax.random.randint(jax.random.fold_in(rng, axis), (), 0, extent[axis]) for axis in range(len(extent))]
    drawn = drawn.at[tuple(spot)].set(low)
    longest = extent.index(max(extent))
    spot[longest] = (spot[longest] + 1) % extent[longest]
    return drawn.at[tuple(spot)].set(top_value)


def block_levels(rng, dims, shards, least, top_value):
    gain = 1.0
    for axis_at, blocks in shards:
        draws = jax.random.uniform(jax.random.fold_in(jax.random.fold_in(rng, 6), axis_at), (blocks,), jnp.float32, least / len(shards), top_value / len(shards))
        gain = gain * jnp.repeat(jnp.exp(draws), dims[axis_at] // blocks).reshape((-1,) + (1,) * (len(dims) - 1 - axis_at))
    return gain


def bell_draw(own_key, shape, spread, limit, cuts=(), kind=jnp.bfloat16):
    drawn = jax.random.normal(own_key, shape, jnp.float32) * spread
    if len(cuts) > 0:
        drawn = block_levels(own_key, shape, cuts, -0.22, 0.18) * drawn
    return jnp.clip(drawn, min=-limit, max=limit).astype(kind)


def setup_inputs(seed: int = 0) -> dict:
    seeds = jax.random.split(jax.random.key(seed), 7)
    acts = bell_draw(seeds[0], (N_DP, N_SECTION, MB, TOK, D), 1.0, 6.0, ((0, 8), (1, 4)))
    weight_v = bell_draw(seeds[1], (N_SECTION, D, VW), D ** -0.5, 0.09375, ((0, 4),))
    weight_o = bell_draw(seeds[2], (N_SECTION, VW, D), D ** -0.5, 0.09375, ((0, 4),))
    top_grad = bell_draw(seeds[3], (N_DP, MB, TOK, D), 1.0, 6.0, ((0, 8),))
    loss_mask = with_ends((jax.random.randint(seeds[4], (N_DP, MB, TOK), 0, 4) < 3).astype(jnp.int32), jax.random.fold_in(seeds[4], 1), 0, 1)
    q_prev = bell_draw(seeds[5], (N_SECTION, VW, R), VW ** -0.5, 0.25, ((0, 4),), jnp.float32)
    return {"acts": acts, "weight_v": weight_v, "weight_o": weight_o, "top_grad": top_grad, "loss_mask": loss_mask, "q_prev": q_prev}


def reference(acts, weight_v, weight_o, top_grad, loss_mask, q_prev):
    high = lax.Precision.HIGHEST
    grad_now = (top_grad.astype(jnp.float32) * loss_mask[..., None].astype(jnp.float32)).astype(jnp.bfloat16)
    bases = []
    rights = []
    for section in reversed(range(N_SECTION)):
        inputs = acts[:, section].astype(jnp.float32)
        wv_full = weight_v[section].astype(jnp.float32)
        wo_full = weight_o[section].astype(jnp.float32)
        grad_f = grad_now.astype(jnp.float32)
        dvalue = jnp.einsum('pmtd,vd->pmtv', grad_f, wo_full).astype(jnp.bfloat16)
        dvalue_f = dvalue.astype(jnp.float32)
        passed = (grad_f + jnp.einsum('pmtv,dv->pmtd', dvalue_f, wv_full)).astype(jnp.bfloat16)
        right = q_prev[section]
        left = jnp.einsum('pmtd,pmtr->dr', inputs, jnp.einsum('pmtv,vr->pmtr', dvalue_f, right, precision=high), precision=high)
        left = left / N_DP
        gram = jnp.dot(left.T, left, precision=high)
        lower = jnp.linalg.cholesky(gram)
        unit = lax.linalg.triangular_solve(lower, left, left_side=False, lower=True, transpose_a=True)
        fresh = jnp.einsum('pmtv,pmtr->vr', dvalue_f, jnp.einsum('pmtd,dr->pmtr', inputs, unit, precision=high), precision=high)
        bases.append(unit * math.sqrt(D))
        rights.append(fresh / N_DP)
        grad_now = passed
    return (jnp.stack(bases[::-1]), jnp.stack(rights[::-1]))
```

```python
import functools
import math

import jax
import jax.numpy as jnp
from jax import lax
from jax.experimental import pallas as pl
from jax.experimental.pallas import tpu as pltpu
from jax.sharding import PartitionSpec as P

MESH = pl.DeviceIdType.MESH
CHUNK = 16
BLOCK = 4
F32 = jnp.float32
BF16 = jnp.bfloat16


def dot(a, b, dims):
    return lax.dot_general(a, b, ((dims[0], dims[1]), ((), ())), preferred_element_type=F32)


def halves(value):
    high = value.astype(BF16)
    low = (value - high.astype(F32)).astype(BF16)
    return high, low


def paired(value, axis):
    return jnp.concatenate(halves(value), axis=axis)


def folded(both, axis):
    half = both.shape[axis] // 2
    if axis == 0:
        return both[:half] + both[half:]
    return both[:, :half] + both[:, half:]


def inverse_factor(gram):
    rank = gram.shape[0]
    row_id = lax.broadcasted_iota(jnp.int32, (rank, rank), 0)
    col_id = lax.broadcasted_iota(jnp.int32, (rank, rank), 1)
    eye = (row_id == col_id).astype(F32)
    full = jnp.concatenate([gram, eye], axis=1)
    wide_row = lax.broadcasted_iota(jnp.int32, (rank, 2 * rank), 0)
    for j in range(0, rank, BLOCK):
        cols = [jnp.broadcast_to(full[:, j + i : j + i + 1], (rank, 2 * rank)) for i in range(BLOCK)]
        rows = [full[j + i : j + i + 1, :] for i in range(BLOCK)]
        for i in range(BLOCK):
            inv = 1.0 / cols[i][j + i : j + i + 1, :]
            scaled = rows[i] * inv
            for k in range(i + 1, BLOCK):
                factor = cols[i][j + k : j + k + 1, :]
                rows[k] = rows[k] - factor * scaled
                cols[k] = cols[k] - cols[i] * (factor * inv)
            full = full - jnp.where(wide_row > j + i, cols[i], 0.0) * scaled
    pivots = jnp.sum(jnp.where(row_id == col_id, full[:, :rank], 0.0), axis=1, keepdims=True)
    return full[:, rank:] * (1.0 / jnp.sqrt(pivots))


def relay(
    replicas, sections, acts, wv_hbm, wo_hbm, tg_hbm, mask_hbm, q_hbm, basis, fresh,
    xall, wv, wo, tg, mask, q, gin, gout, dvall, leftall, gramall, wpart, wparts, wsums,
    local_sem, x_send, x_recv, g_send, g_recv, dv_send, dv_recv,
    gram_send, gram_recv, left_send, left_recv, wp_send, wp_recv, ws_send, ws_recv,
):
    me = lax.axis_index("dp")
    here = lax.axis_index("section")
    at_end = here == sections - 1
    at_start = here == 0
    chunks, size, width = gin.shape
    tokens = chunks * size
    piece = xall.shape[2]
    rank, features = q.shape
    share = rank // replicas
    batches, batch_tokens = mask.shape

    def peer(step):
        return lax.rem(me + step, replicas)

    def remote(src, dst, send, recv, target):
        return pltpu.make_async_remote_copy(
            src_ref=src, dst_ref=dst, send_sem=send, recv_sem=recv,
            device_id=target, device_id_type=MESH,
        )

    load_wo = pltpu.make_async_copy(wo_hbm, wo, local_sem.at[0])
    load_wv = pltpu.make_async_copy(wv_hbm, wv, local_sem.at[1])
    load_tg = pltpu.make_async_copy(tg_hbm, tg, local_sem.at[2])
    load_mask = pltpu.make_async_copy(mask_hbm, mask, local_sem.at[3])
    load_q = pltpu.make_async_copy(q_hbm, q, local_sem.at[4])
    own_cols = pl.ds(pl.multiple_of(me * piece, piece), piece)
    load_x = pltpu.make_async_copy(acts.at[:, own_cols], xall.at[me], local_sem.at[5])

    @pl.when(at_end)
    def _():
        load_mask.start()
        load_tg.start()

    load_wo.start()
    load_wv.start()
    load_q.start()
    load_x.start()

    barrier = pltpu.get_barrier_semaphore()
    for step in range(1, replicas):
        pl.semaphore_signal(barrier, inc=1, device_id=(peer(step), here), device_id_type=MESH)

    @pl.when(jnp.logical_not(at_start))
    def _():
        pl.semaphore_signal(barrier, inc=1, device_id=(me, here - 1), device_id_type=MESH)

    @pl.when(jnp.logical_not(at_end))
    def _():
        pl.semaphore_signal(barrier, inc=1, device_id=(me, here + 1), device_id_type=MESH)

    beside = jnp.where(at_start, 0, 1) + jnp.where(at_end, 0, 1)
    pl.semaphore_wait(barrier, replicas - 1 + beside)

    def x_copy(step):
        to = peer(step)
        cols = pl.ds(pl.multiple_of(to * piece, piece), piece)
        return remote(acts.at[:, cols], xall.at[me], x_send.at[step], x_recv.at[me], (to, here))

    for step in range(1, replicas):
        x_copy(step).start()

    @pl.when(at_end)
    def _():
        load_mask.wait()
        load_tg.wait()
        diagonal = lax.broadcasted_iota(jnp.int32, (batch_tokens, batch_tokens), 0) == lax.broadcasted_iota(
            jnp.int32, (batch_tokens, batch_tokens), 1
        )
        per = batch_tokens // size
        for batch in range(batches):
            line = mask[batch : batch + 1, :].astype(F32)
            column = jnp.sum(jnp.where(diagonal, line, 0.0), axis=1, keepdims=True)
            for part in range(per):
                at = batch * per + part
                gin[at] = (tg[at].astype(F32) * column[part * size : (part + 1) * size]).astype(BF16)

    load_wo.wait()

    def g_copy(c):
        return remote(gout.at[c], gin.at[c], g_send.at[c], g_recv.at[c], (me, here - 1))

    def dv_copy(c, step):
        return remote(
            dvall.at[me, c], dvall.at[me, c], dv_send.at[step, c], dv_recv.at[me, c], (peer(step), here)
        )

    load_wv.wait()

    def advance(c, carry):
        @pl.when(jnp.logical_not(at_end))
        def _():
            remote(gin.at[c], gin.at[c], g_send.at[c], g_recv.at[c], (me, here + 1)).wait_recv()

        grad = gin[c]
        dvalue = dot(grad, wo[...], ((1,), (1,))).astype(BF16)
        dvall[me, c] = dvalue

        @pl.when(jnp.logical_not(at_start))
        def _():
            gout[c] = (grad.astype(F32) + dot(dvalue, wv[...], ((1,), (1,)))).astype(BF16)
            g_copy(c).start()

        for step in range(1, replicas):
            dv_copy(c, step).start()
        return carry

    lax.fori_loop(0, chunks, advance, 0)

    load_x.wait()
    load_q.wait()
    for step in range(1, replicas):
        other = peer(step)
        remote(xall.at[other], xall.at[other], x_send.at[step], x_recv.at[other], (other, here)).wait_recv()

    def dv_arrived(c, carry):
        for step in range(1, replicas):
            other = peer(step)
            remote(
                dvall.at[other, c], dvall.at[other, c], dv_send.at[step, c], dv_recv.at[other, c], (other, here)
            ).wait_recv()
        return carry

    lax.fori_loop(0, chunks, dv_arrived, 0)

    everything = xall[...].reshape(replicas * tokens, piece)
    dvalues = dvall[...].reshape(replicas * tokens, features)
    base = folded(dot(dvalues, paired(q[...], 0), ((1,), (1,))), 1)
    left = folded(dot(paired(base, 1), everything, ((0,), (0,))), 0) * (1.0 / replicas)
    gramall[me] = lax.dot_general(
        left, left, (((1,), (1,)), ((), ())), precision=lax.Precision.HIGHEST, preferred_element_type=F32
    )

    def gram_copy(step):
        return remote(gramall.at[me], gramall.at[me], gram_send.at[step], gram_recv.at[me], (peer(step), here))

    for step in range(1, replicas):
        gram_copy(step).start()
    leftall[me] = left.astype(BF16)

    def left_copy(step):
        return remote(leftall.at[me], leftall.at[me], left_send.at[step], left_recv.at[me], (peer(step), here))

    response = folded(dot(everything, paired(left, 0), ((1,), (1,))), 1)
    wpart[...] = folded(dot(paired(response, 1), dvalues, ((0,), (0,))), 0).reshape(replicas, share, features)

    def wp_copy(step):
        to = peer(step)
        return remote(wpart.at[to], wparts.at[me], wp_send.at[step], wp_recv.at[me], (to, here))

    for step in range(1, replicas):
        wp_copy(step).start()
    for step in range(1, replicas):
        left_copy(step).start()
    wparts[me] = wpart[me]

    for step in range(1, replicas):
        other = peer(step)
        remote(gramall.at[other], gramall.at[other], gram_send.at[step], gram_recv.at[other], (other, here)).wait_recv()
    for step in range(1, replicas):
        other = peer(step)
        remote(wparts.at[other], wparts.at[other], wp_send.at[step], wp_recv.at[other], (other, here)).wait_recv()
    total = wparts[0]
    for index in range(1, replicas):
        total = total + wparts[index]
    wsums[me] = total * (1.0 / replicas)

    def ws_copy(step):
        return remote(wsums.at[me], wsums.at[me], ws_send.at[step], ws_recv.at[me], (peer(step), here))

    for step in range(1, replicas):
        ws_copy(step).start()

    gram = gramall[0]
    for index in range(1, replicas):
        gram = gram + gramall[index]
    inverse = inverse_factor(gram)
    factors = paired(inverse, 0)

    for step in range(1, replicas):
        other = peer(step)
        remote(leftall.at[other], leftall.at[other], left_send.at[step], left_recv.at[other], (other, here)).wait_recv()
    scale = math.sqrt(width)
    for index in range(replicas):
        basis[:, index * piece : (index + 1) * piece] = (
            folded(dot(factors, leftall[index], ((1,), (0,))), 0) * scale
        )

    for step in range(1, replicas):
        other = peer(step)
        remote(wsums.at[other], wsums.at[other], ws_send.at[step], ws_recv.at[other], (other, here)).wait_recv()
    fresh[...] = lax.dot_general(
        inverse, wsums[...].reshape(rank, features), (((1,), (0,)), ((), ())),
        precision=lax.Precision.HIGHEST, preferred_element_type=F32,
    )

    for step in range(1, replicas):
        x_copy(step).wait_send()
        gram_copy(step).wait_send()
        wp_copy(step).wait_send()
        left_copy(step).wait_send()
        ws_copy(step).wait_send()

    def sent(c, carry):
        for step in range(1, replicas):
            dv_copy(c, step).wait_send()

        @pl.when(jnp.logical_not(at_start))
        def _():
            g_copy(c).wait_send()

        return carry

    lax.fori_loop(0, chunks, sent, 0)


def local_kernel(replicas, sections, acts, weight_v, weight_o, top_grad, loss_mask, q_prev):
    _, _, batches, batch_tokens, width = acts.shape
    tokens = batches * batch_tokens
    _, features, rank = q_prev.shape
    size = CHUNK
    chunks = tokens // size
    piece = width // replicas
    share = rank // replicas
    any_spec = pl.BlockSpec(memory_space=pl.ANY)
    vmem = pl.BlockSpec(memory_space=pltpu.VMEM)
    dma = pltpu.SemaphoreType.DMA
    basis, fresh = pl.pallas_call(
        functools.partial(relay, replicas, sections),
        out_shape=(
            jax.ShapeDtypeStruct((rank, width), F32),
            jax.ShapeDtypeStruct((rank, features), F32),
        ),
        in_specs=[any_spec] * 6,
        out_specs=(vmem, vmem),
        scratch_shapes=[
            pltpu.VMEM((replicas, tokens, piece), BF16),
            pltpu.VMEM((width, features), BF16),
            pltpu.VMEM((features, width), BF16),
            pltpu.VMEM((chunks, size, width), BF16),
            pltpu.VMEM((batches, batch_tokens), jnp.int32),
            pltpu.VMEM((rank, features), F32),
            pltpu.VMEM((chunks, size, width), BF16),
            pltpu.VMEM((chunks, size, width), BF16),
            pltpu.VMEM((replicas, chunks, size, features), BF16),
            pltpu.VMEM((replicas, rank, piece), BF16),
            pltpu.VMEM((replicas, rank, rank), F32),
            pltpu.VMEM((replicas, share, features), F32),
            pltpu.VMEM((replicas, share, features), F32),
            pltpu.VMEM((replicas, share, features), F32),
            dma((6,)),
            dma((replicas,)), dma((replicas,)),
            dma((chunks,)), dma((chunks,)),
            dma((replicas, chunks)), dma((replicas, chunks)),
            dma((replicas,)), dma((replicas,)),
            dma((replicas,)), dma((replicas,)),
            dma((replicas,)), dma((replicas,)),
            dma((replicas,)), dma((replicas,)),
        ],
        compiler_params=pltpu.CompilerParams(
            collective_id=0, has_side_effects=True, vmem_limit_bytes=60 * 1024 * 1024
        ),
    )(
        acts.reshape(tokens, width), weight_v[0], weight_o[0],
        top_grad.reshape(chunks, size, width), loss_mask[0], q_prev[0].T,
    )
    return (basis.T[None], fresh.T[None])


def passed_along(value, axis, steps):
    count = lax.axis_size(axis)
    initial, last = (max(0, -steps), min(count, count - steps))
    return lax.ppermute(value, axis, [(source, source + steps) for source in range(initial, last)])


def propagate(w_value, w_output, grad_in):
    dvalue = jnp.einsum("td,vd->tv", grad_in, w_output, preferred_element_type=jnp.float32).astype(
        jnp.bfloat16
    )
    passed = (
        grad_in.astype(jnp.float32)
        + jnp.einsum("tv,dv->td", dvalue, w_value, preferred_element_type=jnp.float32)
    ).astype(jnp.bfloat16)
    return (passed, dvalue)


def local(acts, weight_v, weight_o, top_grad, loss_mask, q_prev):
    high = lax.Precision.HIGHEST
    inputs = acts[0, 0]
    w_value = weight_v[0]
    w_output = weight_o[0]
    right = q_prev[0]
    batches, tokens, width = inputs.shape
    features = w_value.shape[1]
    sections = lax.axis_size("section")
    here = lax.axis_index("section")
    at_end = here == sections - 1
    seed = (top_grad[0].astype(jnp.float32) * loss_mask[0][..., None].astype(jnp.float32)).astype(
        jnp.bfloat16
    )
    kept_v = jnp.zeros((batches, tokens, features), jnp.bfloat16)

    def advance(step, carry):
        incoming, kept_d = carry
        batch = step - (sections - 1 - here)
        safe = jnp.clip(batch, 0, batches - 1)
        grad_in = jnp.where(at_end, lax.dynamic_index_in_dim(seed, safe, 0, False), incoming)

        def work(operand):
            passed, dvalue = propagate(w_value, w_output, operand)
            return (passed, lax.dynamic_update_index_in_dim(kept_d, dvalue, safe, 0))

        def rest(operand):
            return (jnp.zeros_like(operand), kept_d)

        active = jnp.logical_and(batch >= 0, batch < batches)
        passed, kept_d = lax.cond(active, work, rest, grad_in)
        incoming = passed_along(passed, "section", -1)
        return (incoming, kept_d)

    start = (jnp.zeros((tokens, width), jnp.bfloat16), kept_v)
    _, kept_d = lax.fori_loop(0, sections + batches - 1, advance, start)
    rows = inputs.reshape(-1, width)
    dvalue = kept_d.reshape(-1, features)
    replicas = lax.axis_size("dp")
    gradient = jnp.einsum("td,tv->dv", rows, dvalue, preferred_element_type=jnp.float32)
    term_left = jnp.dot(gradient, right, precision=high)
    left = lax.psum(term_left, "dp") / replicas
    gram = jnp.dot(left.T, left, precision=high)
    lower = jnp.linalg.cholesky(gram)
    unit = lax.linalg.triangular_solve(lower, left, left_side=False, lower=True, transpose_a=True)
    term_right = jnp.einsum("dv,dr->vr", gradient, unit, precision=high)
    fresh = lax.psum(term_right, "dp") / replicas
    return ((unit * math.sqrt(width))[None], fresh[None])


def solution(mesh):
    placed = (
        P("dp", "section", None, None, None),
        P("section", None, None),
        P("section", None, None),
        P("dp", None, None, None),
        P("dp", None, None),
        P("section", None, None),
    )
    replicas = mesh.shape["dp"]
    sections = mesh.shape["section"]

    def body(acts, weight_v, weight_o, top_grad, loss_mask, q_prev):
        args = (acts, weight_v, weight_o, top_grad, loss_mask, q_prev)
        width, features = weight_v.shape[1:]
        fits = (
            replicas > 1
            and width % (replicas * 128) == 0
            and q_prev.shape[2] % (replicas * 8) == 0
            and acts.shape[3] % CHUNK == 0
            and q_prev.shape[2] % BLOCK == 0
        )
        if fits:
            return local_kernel(replicas, sections, *args)
        return local(*args)

    return jax.shard_map(
        body,
        mesh=mesh,
        in_specs=placed,
        out_specs=(P("section", None, None), P("section", None, None)),
        check_vma=False,
    )
```

```python
import functools
import math

import jax
import jax.numpy as jnp
from jax import lax
from jax.experimental import pallas as pl
from jax.experimental.pallas import tpu as pltpu
from jax.sharding import PartitionSpec as P

MESH = pl.DeviceIdType.MESH
CHUNK = 16
BLOCK = 4
PARTS = 4
F32 = jnp.float32
BF16 = jnp.bfloat16


def dot(a, b, dims):
    return lax.dot_general(a, b, ((dims[0], dims[1]), ((), ())), preferred_element_type=F32)


def halves(value):
    high = value.astype(BF16)
    low = (value - high.astype(F32)).astype(BF16)
    return high, low


def paired(value, axis):
    return jnp.concatenate(halves(value), axis=axis)


def folded(both, axis):
    half = both.shape[axis] // 2
    if axis == 0:
        return both[:half] + both[half:]
    return both[:, :half] + both[:, half:]


def inverse_factor(gram):
    rank = gram.shape[0]
    row_id = lax.broadcasted_iota(jnp.int32, (rank, rank), 0)
    col_id = lax.broadcasted_iota(jnp.int32, (rank, rank), 1)
    eye = (row_id == col_id).astype(F32)
    full = jnp.concatenate([gram, eye], axis=1)
    wide_row = lax.broadcasted_iota(jnp.int32, (rank, 2 * rank), 0)
    for j in range(0, rank, BLOCK):
        cols = [jnp.broadcast_to(full[:, j + i : j + i + 1], (rank, 2 * rank)) for i in range(BLOCK)]
        rows = [full[j + i : j + i + 1, :] for i in range(BLOCK)]
        for i in range(BLOCK):
            inv = 1.0 / cols[i][j + i : j + i + 1, :]
            scaled = rows[i] * inv
            for k in range(i + 1, BLOCK):
                factor = cols[i][j + k : j + k + 1, :]
                rows[k] = rows[k] - factor * scaled
                cols[k] = cols[k] - cols[i] * (factor * inv)
            full = full - jnp.where(wide_row > j + i, cols[i], 0.0) * scaled
    pivots = jnp.sum(jnp.where(row_id == col_id, full[:, :rank], 0.0), axis=1, keepdims=True)
    return full[:, rank:] * (1.0 / jnp.sqrt(pivots))


def relay(
    replicas, sections, acts, wv_hbm, wo_hbm, tg_hbm, mask_hbm, q_hbm, leftall, wsums, inverse_out,
    xall, wv, wo, tg, mask, q, gin, gout, dvall, gramall, wpart, wparts,
    local_sem, wo_sem, wv_sem, x_send, x_recv, g_send, g_recv, dv_send, dv_recv,
    gram_send, gram_recv, left_send, left_recv, wp_send, wp_recv, ws_send, ws_recv,
):
    me = lax.axis_index("dp")
    here = lax.axis_index("section")
    at_end = here == sections - 1
    at_start = here == 0
    chunks, size, width = gin.shape
    tokens = chunks * size
    piece = xall.shape[2]
    rank, features = q.shape
    share = rank // replicas
    batches, batch_tokens = mask.shape

    def peer(step):
        return lax.rem(me + step, replicas)

    def remote(src, dst, send, recv, target):
        return pltpu.make_async_remote_copy(
            src_ref=src, dst_ref=dst, send_sem=send, recv_sem=recv,
            device_id=target, device_id_type=MESH,
        )

    column = width // PARTS

    def load_wo(part):
        cols = pl.ds(part * column, column)
        return pltpu.make_async_copy(wo_hbm.at[:, cols], wo.at[:, cols], wo_sem.at[part])

    def load_wv(part):
        cols = pl.ds(part * column, column)
        return pltpu.make_async_copy(wv_hbm.at[cols], wv.at[cols], wv_sem.at[part])

    load_tg = pltpu.make_async_copy(tg_hbm, tg, local_sem.at[2])
    load_mask = pltpu.make_async_copy(mask_hbm, mask, local_sem.at[3])
    load_q = pltpu.make_async_copy(q_hbm, q, local_sem.at[4])
    own_cols = pl.ds(pl.multiple_of(me * piece, piece), piece)
    load_x = pltpu.make_async_copy(acts.at[:, own_cols], xall.at[me], local_sem.at[5])

    @pl.when(at_end)
    def _():
        load_mask.start()
        load_tg.start()

    for part in range(PARTS):
        load_wo(part).start()
    for part in range(PARTS):
        load_wv(part).start()
    load_q.start()
    load_x.start()

    barrier = pltpu.get_barrier_semaphore()
    for step in range(1, replicas):
        pl.semaphore_signal(barrier, inc=1, device_id=(peer(step), here), device_id_type=MESH)

    @pl.when(jnp.logical_not(at_start))
    def _():
        pl.semaphore_signal(barrier, inc=1, device_id=(me, here - 1), device_id_type=MESH)

    @pl.when(jnp.logical_not(at_end))
    def _():
        pl.semaphore_signal(barrier, inc=1, device_id=(me, here + 1), device_id_type=MESH)

    def x_copy(step):
        to = peer(step)
        cols = pl.ds(pl.multiple_of(to * piece, piece), piece)
        return remote(acts.at[:, cols], xall.at[me], x_send.at[step], x_recv.at[me], (to, here))

    @pl.when(at_end)
    def _():
        load_mask.wait()
        load_tg.wait()
        diagonal = lax.broadcasted_iota(jnp.int32, (batch_tokens, batch_tokens), 0) == lax.broadcasted_iota(
            jnp.int32, (batch_tokens, batch_tokens), 1
        )
        per = batch_tokens // size
        for batch in range(batches):
            line = mask[batch : batch + 1, :].astype(F32)
            keep = jnp.sum(jnp.where(diagonal, line, 0.0), axis=1, keepdims=True)
            for part in range(per):
                at = batch * per + part
                gin[at] = (tg[at].astype(F32) * keep[part * size : (part + 1) * size]).astype(BF16)

    beside = jnp.where(at_start, 0, 1) + jnp.where(at_end, 0, 1)
    pl.semaphore_wait(barrier, replicas - 1 + beside)

    for step in range(1, replicas):
        x_copy(step).start()

    def g_copy(c, part):
        cols = pl.ds(part * column, column)
        return remote(
            gout.at[c, :, cols], gin.at[c, :, cols], g_send.at[c, part], g_recv.at[c, part], (me, here - 1)
        )

    def dv_copy(c, step):
        return remote(
            dvall.at[me, c], dvall.at[me, c], dv_send.at[step, c], dv_recv.at[me, c], (peer(step), here)
        )

    def advance(c, carry):
        total = None
        for part in range(PARTS):
            cols = slice(part * column, (part + 1) * column)
            spot = pl.ds(part * column, column)

            @pl.when(c == 0)
            def _():
                load_wo(part).wait()

            @pl.when(jnp.logical_not(at_end))
            def _():
                remote(
                    gin.at[c, :, spot], gin.at[c, :, spot], g_send.at[c, part], g_recv.at[c, part], (me, here + 1)
                ).wait_recv()

            term = dot(gin[c, :, cols], wo[:, cols], ((1,), (1,)))
            total = term if part == 0 else total + term
        dvalue = total.astype(BF16)
        dvall[me, c] = dvalue

        for part in range(PARTS):
            cols = slice(part * column, (part + 1) * column)

            @pl.when(c == 0)
            def _():
                load_wv(part).wait()

            @pl.when(jnp.logical_not(at_start))
            def _():
                gout[c, :, cols] = (
                    gin[c, :, cols].astype(F32) + dot(dvalue, wv[cols, :], ((1,), (1,)))
                ).astype(BF16)
                g_copy(c, part).start()

        for step in range(1, replicas):
            dv_copy(c, step).start()
        return carry

    lax.fori_loop(0, chunks, advance, 0)

    load_x.wait()
    load_q.wait()
    for step in range(1, replicas):
        other = peer(step)
        remote(xall.at[other], xall.at[other], x_send.at[step], x_recv.at[other], (other, here)).wait_recv()

    def dv_arrived(c, carry):
        for step in range(1, replicas):
            other = peer(step)
            remote(
                dvall.at[other, c], dvall.at[other, c], dv_send.at[step, c], dv_recv.at[other, c], (other, here)
            ).wait_recv()
        return carry

    lax.fori_loop(0, chunks, dv_arrived, 0)

    everything = xall[...].reshape(replicas * tokens, piece)
    dvalues = dvall[...].reshape(replicas * tokens, features)
    base = folded(dot(dvalues, paired(q[...], 0), ((1,), (1,))), 1)
    left = folded(dot(paired(base, 1), everything, ((0,), (0,))), 0) * (1.0 / replicas)
    def gram_copy(step):
        return remote(gramall.at[me], gramall.at[me], gram_send.at[step], gram_recv.at[me], (peer(step), here))

    def left_copy(step):
        return remote(leftall.at[me], leftall.at[me], left_send.at[step], left_recv.at[me], (peer(step), here))

    leftall[me] = left.astype(BF16)
    gramall[me] = lax.dot_general(
        left, left, (((1,), (1,)), ((), ())), precision=lax.Precision.HIGHEST, preferred_element_type=F32
    )
    for step in range(1, replicas):
        gram_copy(step).start()
    for step in range(1, replicas):
        left_copy(step).start()
    response = folded(dot(everything, paired(left, 0), ((1,), (1,))), 1)
    wpart[...] = folded(dot(paired(response, 1), dvalues, ((0,), (0,))), 0).reshape(replicas, share, features)

    def wp_copy(step):
        to = peer(step)
        return remote(wpart.at[to], wparts.at[me], wp_send.at[step], wp_recv.at[me], (to, here))

    for step in range(1, replicas):
        wp_copy(step).start()
    wparts[me] = wpart[me]

    for step in range(1, replicas):
        other = peer(step)
        remote(gramall.at[other], gramall.at[other], gram_send.at[step], gram_recv.at[other], (other, here)).wait_recv()
    for step in range(1, replicas):
        other = peer(step)
        remote(wparts.at[other], wparts.at[other], wp_send.at[step], wp_recv.at[other], (other, here)).wait_recv()
    total = wparts[0]
    for index in range(1, replicas):
        total = total + wparts[index]
    wsums[me] = total * (1.0 / replicas)

    def ws_copy(step):
        return remote(wsums.at[me], wsums.at[me], ws_send.at[step], ws_recv.at[me], (peer(step), here))

    for step in range(1, replicas):
        ws_copy(step).start()

    gram = gramall[0]
    for index in range(1, replicas):
        gram = gram + gramall[index]
    inverse = inverse_factor(gram)
    inverse_out[...] = inverse

    for step in range(1, replicas):
        other = peer(step)
        remote(leftall.at[other], leftall.at[other], left_send.at[step], left_recv.at[other], (other, here)).wait_recv()
    for step in range(1, replicas):
        other = peer(step)
        remote(wsums.at[other], wsums.at[other], ws_send.at[step], ws_recv.at[other], (other, here)).wait_recv()
    for step in range(1, replicas):
        x_copy(step).wait_send()
        gram_copy(step).wait_send()
        wp_copy(step).wait_send()
        left_copy(step).wait_send()
        ws_copy(step).wait_send()

    def sent(c, carry):
        for step in range(1, replicas):
            dv_copy(c, step).wait_send()

        @pl.when(jnp.logical_not(at_start))
        def _():
            for part in range(PARTS):
                g_copy(c, part).wait_send()

        return carry

    lax.fori_loop(0, chunks, sent, 0)


def finish(leftall, wsums, inverse, basis, fresh):
    replicas, rank, piece = leftall.shape
    factors = paired(inverse[...], 0)
    scale = math.sqrt(replicas * piece)
    for index in range(replicas):
        basis[:, index * piece : (index + 1) * piece] = (
            folded(dot(factors, leftall[index], ((1,), (0,))), 0) * scale
        )
    fresh[...] = lax.dot_general(
        inverse[...], wsums[...].reshape(rank, -1), (((1,), (0,)), ((), ())),
        precision=lax.Precision.HIGHEST, preferred_element_type=F32,
    )


def local_kernel(replicas, sections, acts, weight_v, weight_o, top_grad, loss_mask, q_prev):
    _, _, batches, batch_tokens, width = acts.shape
    tokens = batches * batch_tokens
    _, features, rank = q_prev.shape
    size = CHUNK
    chunks = tokens // size
    piece = width // replicas
    share = rank // replicas
    any_spec = pl.BlockSpec(memory_space=pl.ANY)
    vmem = pl.BlockSpec(memory_space=pltpu.VMEM)
    dma = pltpu.SemaphoreType.DMA
    leftall, wsums, inverse = pl.pallas_call(
        functools.partial(relay, replicas, sections),
        out_shape=(
            jax.ShapeDtypeStruct((replicas, rank, piece), BF16),
            jax.ShapeDtypeStruct((replicas, share, features), F32),
            jax.ShapeDtypeStruct((rank, rank), F32),
        ),
        in_specs=[any_spec] * 6,
        out_specs=(vmem, vmem, vmem),
        scratch_shapes=[
            pltpu.VMEM((replicas, tokens, piece), BF16),
            pltpu.VMEM((width, features), BF16),
            pltpu.VMEM((features, width), BF16),
            pltpu.VMEM((chunks, size, width), BF16),
            pltpu.VMEM((batches, batch_tokens), jnp.int32),
            pltpu.VMEM((rank, features), F32),
            pltpu.VMEM((chunks, size, width), BF16),
            pltpu.VMEM((chunks, size, width), BF16),
            pltpu.VMEM((replicas, chunks, size, features), BF16),
            pltpu.VMEM((replicas, rank, rank), F32),
            pltpu.VMEM((replicas, share, features), F32),
            pltpu.VMEM((replicas, share, features), F32),
            dma((6,)), dma((PARTS,)), dma((PARTS,)),
            dma((replicas,)), dma((replicas,)),
            dma((chunks, PARTS)), dma((chunks, PARTS)),
            dma((replicas, chunks)), dma((replicas, chunks)),
            dma((replicas,)), dma((replicas,)),
            dma((replicas,)), dma((replicas,)),
            dma((replicas,)), dma((replicas,)),
            dma((replicas,)), dma((replicas,)),
        ],
        compiler_params=pltpu.CompilerParams(
            collective_id=0, has_side_effects=True, vmem_limit_bytes=60 * 1024 * 1024
        ),
    )(
        acts.reshape(tokens, width), weight_v[0], weight_o[0],
        top_grad.reshape(chunks, size, width), loss_mask[0], q_prev[0].T,
    )
    basis, fresh = pl.pallas_call(
        finish,
        out_shape=(
            jax.ShapeDtypeStruct((rank, width), F32),
            jax.ShapeDtypeStruct((rank, features), F32),
        ),
        in_specs=[vmem] * 3,
        out_specs=(vmem, vmem),
    )(leftall, wsums, inverse)
    return (basis.T[None], fresh.T[None])


def passed_along(value, axis, steps):
    count = lax.axis_size(axis)
    initial, last = (max(0, -steps), min(count, count - steps))
    return lax.ppermute(value, axis, [(source, source + steps) for source in range(initial, last)])


def propagate(w_value, w_output, grad_in):
    dvalue = jnp.einsum("td,vd->tv", grad_in, w_output, preferred_element_type=jnp.float32).astype(
        jnp.bfloat16
    )
    passed = (
        grad_in.astype(jnp.float32)
        + jnp.einsum("tv,dv->td", dvalue, w_value, preferred_element_type=jnp.float32)
    ).astype(jnp.bfloat16)
    return (passed, dvalue)


def local(acts, weight_v, weight_o, top_grad, loss_mask, q_prev):
    high = lax.Precision.HIGHEST
    inputs = acts[0, 0]
    w_value = weight_v[0]
    w_output = weight_o[0]
    right = q_prev[0]
    batches, tokens, width = inputs.shape
    features = w_value.shape[1]
    sections = lax.axis_size("section")
    here = lax.axis_index("section")
    at_end = here == sections - 1
    seed = (top_grad[0].astype(jnp.float32) * loss_mask[0][..., None].astype(jnp.float32)).astype(
        jnp.bfloat16
    )
    kept_v = jnp.zeros((batches, tokens, features), jnp.bfloat16)

    def advance(step, carry):
        incoming, kept_d = carry
        batch = step - (sections - 1 - here)
        safe = jnp.clip(batch, 0, batches - 1)
        grad_in = jnp.where(at_end, lax.dynamic_index_in_dim(seed, safe, 0, False), incoming)

        def work(operand):
            passed, dvalue = propagate(w_value, w_output, operand)
            return (passed, lax.dynamic_update_index_in_dim(kept_d, dvalue, safe, 0))

        def rest(operand):
            return (jnp.zeros_like(operand), kept_d)

        active = jnp.logical_and(batch >= 0, batch < batches)
        passed, kept_d = lax.cond(active, work, rest, grad_in)
        incoming = passed_along(passed, "section", -1)
        return (incoming, kept_d)

    start = (jnp.zeros((tokens, width), jnp.bfloat16), kept_v)
    _, kept_d = lax.fori_loop(0, sections + batches - 1, advance, start)
    rows = inputs.reshape(-1, width)
    dvalue = kept_d.reshape(-1, features)
    replicas = lax.axis_size("dp")
    gradient = jnp.einsum("td,tv->dv", rows, dvalue, preferred_element_type=jnp.float32)
    term_left = jnp.dot(gradient, right, precision=high)
    left = lax.psum(term_left, "dp") / replicas
    gram = jnp.dot(left.T, left, precision=high)
    lower = jnp.linalg.cholesky(gram)
    unit = lax.linalg.triangular_solve(lower, left, left_side=False, lower=True, transpose_a=True)
    term_right = jnp.einsum("dv,dr->vr", gradient, unit, precision=high)
    fresh = lax.psum(term_right, "dp") / replicas
    return ((unit * math.sqrt(width))[None], fresh[None])


def solution(mesh):
    placed = (
        P("dp", "section", None, None, None),
        P("section", None, None),
        P("section", None, None),
        P("dp", None, None, None),
        P("dp", None, None),
        P("section", None, None),
    )
    replicas = mesh.shape["dp"]
    sections = mesh.shape["section"]

    def body(acts, weight_v, weight_o, top_grad, loss_mask, q_prev):
        args = (acts, weight_v, weight_o, top_grad, loss_mask, q_prev)
        width, features = weight_v.shape[1:]
        fits = (
            replicas > 1
            and width % (replicas * 128) == 0
            and width % (PARTS * 128) == 0
            and q_prev.shape[2] % (replicas * 8) == 0
            and acts.shape[3] % CHUNK == 0
            and q_prev.shape[2] % BLOCK == 0
        )
        if fits:
            return local_kernel(replicas, sections, *args)
        return local(*args)

    return jax.shard_map(
        body,
        mesh=mesh,
        in_specs=placed,
        out_specs=(P("section", None, None), P("section", None, None)),
        check_vma=False,
    )
```

```python
import functools
import math

import jax
import jax.numpy as jnp
from jax import lax
from jax.experimental import pallas as pl
from jax.experimental.pallas import tpu as pltpu
from jax.sharding import PartitionSpec as P

MESH = pl.DeviceIdType.MESH
CHUNK = 16
BLOCK = 4
PARTS = 4
GROUPS = 2
F32 = jnp.float32
BF16 = jnp.bfloat16


def dot(a, b, dims):
    return lax.dot_general(a, b, ((dims[0], dims[1]), ((), ())), preferred_element_type=F32)


def halves(value):
    high = value.astype(BF16)
    low = (value - high.astype(F32)).astype(BF16)
    return high, low


def paired(value, axis):
    return jnp.concatenate(halves(value), axis=axis)


def folded(both, axis):
    half = both.shape[axis] // 2
    if axis == 0:
        return both[:half] + both[half:]
    return both[:, :half] + both[:, half:]


def inverse_factor(gram):
    rank = gram.shape[0]
    row_id = lax.broadcasted_iota(jnp.int32, (rank, rank), 0)
    col_id = lax.broadcasted_iota(jnp.int32, (rank, rank), 1)
    eye = (row_id == col_id).astype(F32)
    full = jnp.concatenate([gram, eye], axis=1)
    wide_row = lax.broadcasted_iota(jnp.int32, (rank, 2 * rank), 0)
    for j in range(0, rank, BLOCK):
        cols = [jnp.broadcast_to(full[:, j + i : j + i + 1], (rank, 2 * rank)) for i in range(BLOCK)]
        rows = [full[j + i : j + i + 1, :] for i in range(BLOCK)]
        for i in range(BLOCK):
            inv = 1.0 / cols[i][j + i : j + i + 1, :]
            scaled = rows[i] * inv
            for k in range(i + 1, BLOCK):
                factor = cols[i][j + k : j + k + 1, :]
                rows[k] = rows[k] - factor * scaled
                cols[k] = cols[k] - cols[i] * (factor * inv)
            full = full - jnp.where(wide_row > j + i, cols[i], 0.0) * scaled
    pivots = jnp.sum(jnp.where(row_id == col_id, full[:, :rank], 0.0), axis=1, keepdims=True)
    return full[:, rank:] * (1.0 / jnp.sqrt(pivots))


def relay(
    replicas, sections, acts, wv_hbm, wo_hbm, tg_hbm, mask_hbm, q_hbm, leftall, wsums, inverse_out,
    xall, wv, wo, tg, mask, q, gin, gout, dvall, gramall, wpart, wparts,
    local_sem, wo_sem, wv_sem, x_send, x_recv, g_send, g_recv, dv_send, dv_recv,
    gram_send, gram_recv, left_send, left_recv, wp_send, wp_recv, ws_send, ws_recv,
):
    me = lax.axis_index("dp")
    here = lax.axis_index("section")
    at_end = here == sections - 1
    at_start = here == 0
    chunks, size, width = gin.shape
    tokens = chunks * size
    piece = xall.shape[2]
    rank, features = q.shape
    share = rank // replicas
    batches, batch_tokens = mask.shape

    def peer(step):
        return lax.rem(me + step, replicas)

    def remote(src, dst, send, recv, target):
        return pltpu.make_async_remote_copy(
            src_ref=src, dst_ref=dst, send_sem=send, recv_sem=recv,
            device_id=target, device_id_type=MESH,
        )

    column = width // PARTS

    def load_wo(part):
        cols = pl.ds(part * column, column)
        return pltpu.make_async_copy(wo_hbm.at[:, cols], wo.at[:, cols], wo_sem.at[part])

    def load_wv(part):
        cols = pl.ds(part * column, column)
        return pltpu.make_async_copy(wv_hbm.at[cols], wv.at[cols], wv_sem.at[part])

    load_tg = pltpu.make_async_copy(tg_hbm, tg, local_sem.at[2])
    load_mask = pltpu.make_async_copy(mask_hbm, mask, local_sem.at[3])
    load_q = pltpu.make_async_copy(q_hbm, q, local_sem.at[4])
    own_cols = pl.ds(pl.multiple_of(me * piece, piece), piece)
    load_x = pltpu.make_async_copy(acts.at[:, own_cols], xall.at[me], local_sem.at[5])

    @pl.when(at_end)
    def _():
        load_mask.start()
        load_tg.start()

    for part in range(PARTS):
        load_wo(part).start()
    for part in range(PARTS):
        load_wv(part).start()
    load_q.start()
    load_x.start()

    barrier = pltpu.get_barrier_semaphore()
    for step in range(1, replicas):
        pl.semaphore_signal(barrier, inc=1, device_id=(peer(step), here), device_id_type=MESH)

    @pl.when(jnp.logical_not(at_start))
    def _():
        pl.semaphore_signal(barrier, inc=1, device_id=(me, here - 1), device_id_type=MESH)

    @pl.when(jnp.logical_not(at_end))
    def _():
        pl.semaphore_signal(barrier, inc=1, device_id=(me, here + 1), device_id_type=MESH)

    def x_copy(step):
        to = peer(step)
        cols = pl.ds(pl.multiple_of(to * piece, piece), piece)
        return remote(acts.at[:, cols], xall.at[me], x_send.at[step], x_recv.at[me], (to, here))

    @pl.when(at_end)
    def _():
        load_mask.wait()
        load_tg.wait()
        diagonal = lax.broadcasted_iota(jnp.int32, (batch_tokens, batch_tokens), 0) == lax.broadcasted_iota(
            jnp.int32, (batch_tokens, batch_tokens), 1
        )
        per = batch_tokens // size
        for batch in range(batches):
            line = mask[batch : batch + 1, :].astype(F32)
            keep = jnp.sum(jnp.where(diagonal, line, 0.0), axis=1, keepdims=True)
            for part in range(per):
                at = batch * per + part
                gin[at] = (tg[at].astype(F32) * keep[part * size : (part + 1) * size]).astype(BF16)

    beside = jnp.where(at_start, 0, 1) + jnp.where(at_end, 0, 1)
    pl.semaphore_wait(barrier, replicas - 1 + beside)

    for step in range(1, replicas):
        x_copy(step).start()

    def g_copy(c, part):
        cols = pl.ds(part * column, column)
        return remote(
            gout.at[c, :, cols], gin.at[c, :, cols], g_send.at[c, part], g_recv.at[c, part], (me, here - 1)
        )

    def dv_copy(c, step):
        return remote(
            dvall.at[me, c], dvall.at[me, c], dv_send.at[step, c], dv_recv.at[me, c], (peer(step), here)
        )

    for part in range(PARTS):
        load_wo(part).wait()
        load_wv(part).wait()

    def advance(c, carry):
        total = None
        for group in range(GROUPS):
            per_group = PARTS // GROUPS

            @pl.when(jnp.logical_not(at_end))
            def _():
                for part in range(group * per_group, (group + 1) * per_group):
                    spot = pl.ds(part * column, column)
                    remote(
                        gin.at[c, :, spot], gin.at[c, :, spot], g_send.at[c, part], g_recv.at[c, part],
                        (me, here + 1),
                    ).wait_recv()

            cols = slice(group * per_group * column, (group + 1) * per_group * column)
            term = dot(gin[c, :, cols], wo[:, cols], ((1,), (1,)))
            total = term if group == 0 else total + term
        dvalue = total.astype(BF16)
        dvall[me, c] = dvalue

        @pl.when(jnp.logical_not(at_start))
        def _():
            for part in range(PARTS):
                cols = slice(part * column, (part + 1) * column)
                gout[c, :, cols] = (
                    gin[c, :, cols].astype(F32) + dot(dvalue, wv[cols, :], ((1,), (1,)))
                ).astype(BF16)
                g_copy(c, part).start()

        for step in range(1, replicas):
            dv_copy(c, step).start()
        return carry

    lax.fori_loop(0, chunks, advance, 0)

    load_x.wait()
    load_q.wait()
    for step in range(1, replicas):
        other = peer(step)
        remote(xall.at[other], xall.at[other], x_send.at[step], x_recv.at[other], (other, here)).wait_recv()

    def dv_arrived(c, carry):
        for step in range(1, replicas):
            other = peer(step)
            remote(
                dvall.at[other, c], dvall.at[other, c], dv_send.at[step, c], dv_recv.at[other, c], (other, here)
            ).wait_recv()
        return carry

    lax.fori_loop(0, chunks, dv_arrived, 0)

    everything = xall[...].reshape(replicas * tokens, piece)
    dvalues = dvall[...].reshape(replicas * tokens, features)
    base = folded(dot(dvalues, paired(q[...], 0), ((1,), (1,))), 1)
    left = folded(dot(paired(base, 1), everything, ((0,), (0,))), 0) * (1.0 / replicas)
    def gram_copy(step):
        return remote(gramall.at[me], gramall.at[me], gram_send.at[step], gram_recv.at[me], (peer(step), here))

    def left_copy(step):
        return remote(leftall.at[me], leftall.at[me], left_send.at[step], left_recv.at[me], (peer(step), here))

    leftall[me] = left.astype(BF16)
    gramall[me] = lax.dot_general(
        left, left, (((1,), (1,)), ((), ())), precision=lax.Precision.HIGHEST, preferred_element_type=F32
    )
    for step in range(1, replicas):
        gram_copy(step).start()
    for step in range(1, replicas):
        left_copy(step).start()
    response = folded(dot(everything, paired(left, 0), ((1,), (1,))), 1)
    wpart[...] = folded(dot(paired(response, 1), dvalues, ((0,), (0,))), 0).reshape(replicas, share, features)

    def wp_copy(step):
        to = peer(step)
        return remote(wpart.at[to], wparts.at[me], wp_send.at[step], wp_recv.at[me], (to, here))

    for step in range(1, replicas):
        wp_copy(step).start()
    wparts[me] = wpart[me]

    for step in range(1, replicas):
        other = peer(step)
        remote(gramall.at[other], gramall.at[other], gram_send.at[step], gram_recv.at[other], (other, here)).wait_recv()
    for step in range(1, replicas):
        other = peer(step)
        remote(wparts.at[other], wparts.at[other], wp_send.at[step], wp_recv.at[other], (other, here)).wait_recv()
    total = wparts[0]
    for index in range(1, replicas):
        total = total + wparts[index]
    wsums[me] = total * (1.0 / replicas)

    def ws_copy(step):
        return remote(wsums.at[me], wsums.at[me], ws_send.at[step], ws_recv.at[me], (peer(step), here))

    for step in range(1, replicas):
        ws_copy(step).start()

    gram = gramall[0]
    for index in range(1, replicas):
        gram = gram + gramall[index]
    inverse = inverse_factor(gram)
    inverse_out[...] = inverse

    for step in range(1, replicas):
        other = peer(step)
        remote(leftall.at[other], leftall.at[other], left_send.at[step], left_recv.at[other], (other, here)).wait_recv()
    for step in range(1, replicas):
        other = peer(step)
        remote(wsums.at[other], wsums.at[other], ws_send.at[step], ws_recv.at[other], (other, here)).wait_recv()
    for step in range(1, replicas):
        x_copy(step).wait_send()
        gram_copy(step).wait_send()
        wp_copy(step).wait_send()
        left_copy(step).wait_send()
        ws_copy(step).wait_send()

    def sent(c, carry):
        for step in range(1, replicas):
            dv_copy(c, step).wait_send()

        @pl.when(jnp.logical_not(at_start))
        def _():
            for part in range(PARTS):
                g_copy(c, part).wait_send()

        return carry

    lax.fori_loop(0, chunks, sent, 0)


def finish(leftall, wsums, inverse, basis, fresh):
    replicas, rank, piece = leftall.shape
    factors = paired(inverse[...], 0)
    scale = math.sqrt(replicas * piece)
    for index in range(replicas):
        basis[:, index * piece : (index + 1) * piece] = (
            folded(dot(factors, leftall[index], ((1,), (0,))), 0) * scale
        )
    fresh[...] = lax.dot_general(
        inverse[...], wsums[...].reshape(rank, -1), (((1,), (0,)), ((), ())),
        precision=lax.Precision.HIGHEST, preferred_element_type=F32,
    )


def local_kernel(replicas, sections, acts, weight_v, weight_o, top_grad, loss_mask, q_prev):
    _, _, batches, batch_tokens, width = acts.shape
    tokens = batches * batch_tokens
    _, features, rank = q_prev.shape
    size = CHUNK
    chunks = tokens // size
    piece = width // replicas
    share = rank // replicas
    any_spec = pl.BlockSpec(memory_space=pl.ANY)
    vmem = pl.BlockSpec(memory_space=pltpu.VMEM)
    dma = pltpu.SemaphoreType.DMA
    leftall, wsums, inverse = pl.pallas_call(
        functools.partial(relay, replicas, sections),
        out_shape=(
            jax.ShapeDtypeStruct((replicas, rank, piece), BF16),
            jax.ShapeDtypeStruct((replicas, share, features), F32),
            jax.ShapeDtypeStruct((rank, rank), F32),
        ),
        in_specs=[any_spec] * 6,
        out_specs=(vmem, vmem, vmem),
        scratch_shapes=[
            pltpu.VMEM((replicas, tokens, piece), BF16),
            pltpu.VMEM((width, features), BF16),
            pltpu.VMEM((features, width), BF16),
            pltpu.VMEM((chunks, size, width), BF16),
            pltpu.VMEM((batches, batch_tokens), jnp.int32),
            pltpu.VMEM((rank, features), F32),
            pltpu.VMEM((chunks, size, width), BF16),
            pltpu.VMEM((chunks, size, width), BF16),
            pltpu.VMEM((replicas, chunks, size, features), BF16),
            pltpu.VMEM((replicas, rank, rank), F32),
            pltpu.VMEM((replicas, share, features), F32),
            pltpu.VMEM((replicas, share, features), F32),
            dma((6,)), dma((PARTS,)), dma((PARTS,)),
            dma((replicas,)), dma((replicas,)),
            dma((chunks, PARTS)), dma((chunks, PARTS)),
            dma((replicas, chunks)), dma((replicas, chunks)),
            dma((replicas,)), dma((replicas,)),
            dma((replicas,)), dma((replicas,)),
            dma((replicas,)), dma((replicas,)),
            dma((replicas,)), dma((replicas,)),
        ],
        compiler_params=pltpu.CompilerParams(
            collective_id=0, has_side_effects=True, vmem_limit_bytes=60 * 1024 * 1024
        ),
    )(
        acts.reshape(tokens, width), weight_v[0], weight_o[0],
        top_grad.reshape(chunks, size, width), loss_mask[0], q_prev[0].T,
    )
    basis, fresh = pl.pallas_call(
        finish,
        out_shape=(
            jax.ShapeDtypeStruct((rank, width), F32),
            jax.ShapeDtypeStruct((rank, features), F32),
        ),
        in_specs=[vmem] * 3,
        out_specs=(vmem, vmem),
    )(leftall, wsums, inverse)
    return (basis.T[None], fresh.T[None])


def passed_along(value, axis, steps):
    count = lax.axis_size(axis)
    initial, last = (max(0, -steps), min(count, count - steps))
    return lax.ppermute(value, axis, [(source, source + steps) for source in range(initial, last)])


def propagate(w_value, w_output, grad_in):
    dvalue = jnp.einsum("td,vd->tv", grad_in, w_output, preferred_element_type=jnp.float32).astype(
        jnp.bfloat16
    )
    passed = (
        grad_in.astype(jnp.float32)
        + jnp.einsum("tv,dv->td", dvalue, w_value, preferred_element_type=jnp.float32)
    ).astype(jnp.bfloat16)
    return (passed, dvalue)


def local(acts, weight_v, weight_o, top_grad, loss_mask, q_prev):
    high = lax.Precision.HIGHEST
    inputs = acts[0, 0]
    w_value = weight_v[0]
    w_output = weight_o[0]
    right = q_prev[0]
    batches, tokens, width = inputs.shape
    features = w_value.shape[1]
    sections = lax.axis_size("section")
    here = lax.axis_index("section")
    at_end = here == sections - 1
    seed = (top_grad[0].astype(jnp.float32) * loss_mask[0][..., None].astype(jnp.float32)).astype(
        jnp.bfloat16
    )
    kept_v = jnp.zeros((batches, tokens, features), jnp.bfloat16)

    def advance(step, carry):
        incoming, kept_d = carry
        batch = step - (sections - 1 - here)
        safe = jnp.clip(batch, 0, batches - 1)
        grad_in = jnp.where(at_end, lax.dynamic_index_in_dim(seed, safe, 0, False), incoming)

        def work(operand):
            passed, dvalue = propagate(w_value, w_output, operand)
            return (passed, lax.dynamic_update_index_in_dim(kept_d, dvalue, safe, 0))

        def rest(operand):
            return (jnp.zeros_like(operand), kept_d)

        active = jnp.logical_and(batch >= 0, batch < batches)
        passed, kept_d = lax.cond(active, work, rest, grad_in)
        incoming = passed_along(passed, "section", -1)
        return (incoming, kept_d)

    start = (jnp.zeros((tokens, width), jnp.bfloat16), kept_v)
    _, kept_d = lax.fori_loop(0, sections + batches - 1, advance, start)
    rows = inputs.reshape(-1, width)
    dvalue = kept_d.reshape(-1, features)
    replicas = lax.axis_size("dp")
    gradient = jnp.einsum("td,tv->dv", rows, dvalue, preferred_element_type=jnp.float32)
    term_left = jnp.dot(gradient, right, precision=high)
    left = lax.psum(term_left, "dp") / replicas
    gram = jnp.dot(left.T, left, precision=high)
    lower = jnp.linalg.cholesky(gram)
    unit = lax.linalg.triangular_solve(lower, left, left_side=False, lower=True, transpose_a=True)
    term_right = jnp.einsum("dv,dr->vr", gradient, unit, precision=high)
    fresh = lax.psum(term_right, "dp") / replicas
    return ((unit * math.sqrt(width))[None], fresh[None])


def solution(mesh):
    placed = (
        P("dp", "section", None, None, None),
        P("section", None, None),
        P("section", None, None),
        P("dp", None, None, None),
        P("dp", None, None),
        P("section", None, None),
    )
    replicas = mesh.shape["dp"]
    sections = mesh.shape["section"]

    def body(acts, weight_v, weight_o, top_grad, loss_mask, q_prev):
        args = (acts, weight_v, weight_o, top_grad, loss_mask, q_prev)
        width, features = weight_v.shape[1:]
        fits = (
            replicas > 1
            and width % (replicas * 128) == 0
            and width % (PARTS * 128) == 0
            and q_prev.shape[2] % (replicas * 8) == 0
            and acts.shape[3] % CHUNK == 0
            and q_prev.shape[2] % BLOCK == 0
        )
        if fits:
            return local_kernel(replicas, sections, *args)
        return local(*args)

    return jax.shard_map(
        body,
        mesh=mesh,
        in_specs=placed,
        out_specs=(P("section", None, None), P("section", None, None)),
        check_vma=False,
    )
```
